32 devices in a mesh: grp: 4 (over y, x), ep: 8 (over z, core).
Axes of the slice: x: 2, y: 2, z: 4, core: 2. Of those that a mesh axis runs over, the one named last changes fastest.
Arguments:
- layer_in: bfloat16 [4096, 1536], P(('grp', 'ep')), may hold values from -6 to 6
- segments: int32 [4096], P(('grp', 'ep')), may hold values from 0 to 4, as said below
- routes: int32 [4096, 8], P(('grp', 'ep')), may hold values from 0 to 23, all different within a row; in each aligned block of 128 rows (0 to 127, 128 to 255, ...) at most 56 rows name the same one
- qkv_weight: bfloat16 [2560, 1536], P('ep'), may hold values from -0.15625 to 0.15625
- out_weight: bfloat16 [1536, 1536], P('ep'), may hold values from -1.25 to 1.25
- router_weight: bfloat16 [24, 1536], P('ep'), may hold values from -0.078125 to 0.078125
- norm1_gain: bfloat16 [1536], P('ep'), may hold values from 0.25 to 1.75
- norm2_gain: bfloat16 [1536], P('ep'), may hold values from 0.25 to 1.75
- w_gate: bfloat16 [24, 512, 1536], P('ep'), may hold values from -0.15625 to 0.15625
- w_up: bfloat16 [24, 512, 1536], P('ep'), may hold values from -0.15625 to 0.15625
- w_down: bfloat16 [24, 512, 1536], P('ep'), may hold values from -1 to 1
- out_cotangent: bfloat16 [4096, 1536], P(('grp', 'ep')), may hold values from -6 to 6
Outputs:
- layer_out: bfloat16 [4096, 1536], P(('grp', 'ep'))
- grad_in: bfloat16 [4096, 1536], P(('grp', 'ep'))
- grad_qkv: float32 [2560, 1536], P('ep')
- grad_out_weight: float32 [1536, 1536], P('ep')
- grad_router: float32 [24, 1536], P('ep')
- grad_norm1: float32 [1536], P('ep')
- grad_norm2: float32 [1536], P('ep')
- grad_gate: float32 [24, 512, 1536], P('ep', None, 'grp')
- grad_up: float32 [24, 512, 1536], P('ep', None, 'grp')
- grad_down: float32 [24, 512, 1536], P('ep', None, 'grp')
The draws below stay inside these ranges and needn't reach their ends.
Inputs may be any that keep to these rules, and one draw needn't show every extreme that they name: `segments`: within each sequence of 1024 tokens the numbers start at 0 and rise by one at each new document. Every document has at most 800 tokens and each sequence holds one of exactly 800; every document but a sequence's last has 60 or more. `routes`: each row names 8 different experts. In the rows of one device (128 aligned rows) no expert is named by more than 56 rows, a bound that some block reaches.
All inputs are finite; a program needn't handle non-finite values.
Results may differ from the reference program's by a relative error of at most 0.025.
Values may be sent and summed in bfloat16 or wider, within the bound.
No kernel may reach another device: no remote copies, remote signals or barrier semaphores. Data moves between devices by JAX's collectives and lax.ppermute only.
A program may use at most 192 MiB of HBM per device.

```python
import math
import jax
import jax.numpy as jnp
import numpy as np
from jax import lax

D = 1536
QUERY_HEADS = 24
KEY_VALUE_HEADS = 8
HEAD_DIMENSION = 64
FFE = 512
TOPK = 8
TOK_DEV = 128
DOC_MIN = 60
DOC_MAX = 800
QW = 1536
QKW = 2560
EXPERTS = 24
SEQUENCE_TOKENS = 1024
SEQS = 4
TOKENS = 4096
SEND = 56
CAP = 384


def draw_segments(key, part):
    count = SEQUENCE_TOKENS // DOC_MIN + 2
    key_matrix = jax.random.split(key, 3)
    sizes = jax.random.randint(key_matrix[0], (SEQS, count), DOC_MIN, DOC_MAX + 1)
    which = jax.random.randint(key_matrix[1], (SEQS,), 0, 2)
    opening = jax.random.randint(key_matrix[2], (SEQS,), DOC_MIN, SEQUENCE_TOKENS - DOC_MAX + 1)
    row = jnp.arange(SEQS)[:, None]
    column = jnp.arange(count)[None, :]
    which = jnp.where(jnp.arange(SEQS) == 0, 0, which)
    sizes = jnp.where((row == 0) & (column >= 1), DOC_MIN, sizes)
    sizes = jnp.where(column == which[:, None], DOC_MAX, sizes)
    sizes = jnp.where((column == 0) & (which[:, None] == 1), opening[:, None], sizes)
    ends = jnp.cumsum(sizes, axis=1)
    position = jnp.arange(SEQUENCE_TOKENS)
    numbers = jnp.sum((position[None, :, None] >= ends[:, None, :]).astype(jnp.int32), axis=2)
    return numbers.reshape(SEQS * SEQUENCE_TOKENS).astype(jnp.int32)


def shard_levels(rng, extent, shards, low, high):
    level = 1.0
    for dim, parts in shards:
        heights = jax.random.uniform(jax.random.fold_in(jax.random.fold_in(rng, 6), dim), (parts,), jnp.float32, low / len(shards), high / len(shards))
        level = level * jnp.repeat(jnp.exp(heights), extent[dim] // parts).reshape((-1,) + (1,) * (len(extent) - 1 - dim))
    return level


def deal_out(key, own, number, rows, number_of, top, limit, skew):
    order = jax.random.permutation(key, number_of)
    packed, usual = load_shares(number_of, rows * top, limit, skew, True), load_shares(number_of, rows * top, limit, skew, False)
    places = jnp.arange(number_of)

    def named(tallies, rotation):
        used = int((tallies > 0).sum())
        fixed = max(1, used // 4)
        passed = fixed + (places - fixed + rotation * (used - fixed)) % max(1, number_of - fixed)
        return jnp.zeros((number_of,), jnp.int32).at[order[jnp.where(places < fixed, places, passed)]].set(jnp.asarray(tallies, jnp.int32))

    tallies = jnp.where(number % 4 == 0, named(packed, number // 4), named(usual, number - number // 4 - 1))
    mixed = jax.random.permutation(jax.random.fold_in(own, 3), number_of)
    giver, receiver = mixed[0:number_of // 2 * 2:2], mixed[1:number_of // 2 * 2:2]
    slack = jnp.minimum(tallies[giver] - 1, limit - tallies[receiver]) // 2
    slack = jnp.where((giver == order[0]) | (receiver == order[0]) | (tallies[receiver] == 0), 0, jnp.maximum(slack, 0))
    passed = jax.random.randint(jax.random.fold_in(own, 4), (number_of // 2,), 0, 1 << 20) % (slack + 1)
    tallies = tallies.at[giver].add(-passed).at[receiver].add(passed)
    labels = jnp.searchsorted(jnp.cumsum(tallies), jnp.arange(rows * top), side="right").astype(jnp.int32)
    grid = labels.reshape(top, rows).T
    grid = grid[jax.random.permutation(jax.random.fold_in(own, 1), rows)]
    rotation = jax.random.randint(jax.random.fold_in(own, 2), (rows, 1), 0, top)
    return jnp.take_along_axis(grid, (jnp.arange(top)[None, :] + rotation) % top, axis=1)


def load_shares(number_of, total, bound, skew, full):
    portions = [(1 << 20) // math.isqrt(rank ** skew) + 1 for rank in range(1, number_of + 1)]
    largest = bound if full else min(bound, max(-(-total // number_of), total * portions[0] // sum(portions)))
    least = 1 if total - largest >= number_of - 1 else 0
    given, surplus = [largest] + [least] * (number_of - 1), total - largest - least * (number_of - 1)
    while surplus > 0:
        movable = [i for i in range(1, number_of) if given[i] < largest] or [i for i in range(1, number_of) if given[i] < bound]
        mass, budget = sum([portions[i] for i in movable]), surplus
        for i in movable:
            extra = min(bound - given[i], max(1, budget * portions[i] // mass), surplus)
            given[i] = given[i] + extra
            surplus = surplus - extra
    return np.array(given)


def noise(key, dims, scale, reach, cuts=(), held_as=jnp.bfloat16):
    array = jax.random.normal(key, dims, jnp.float32) * scale
    if len(cuts) > 0:
        array = shard_levels(key, dims, cuts, -0.22, 0.18) * array
    return jnp.clip(array, min=-reach, max=reach).astype(held_as)


def setup_inputs(seed: int = 0) -> dict:
    key_of = jax.random.split(jax.random.key(seed), 13)
    layer_in = noise(key_of[0], (TOKENS, D), 1.0, 6.0, ((0, 32),))
    segments = draw_segments(jax.random.fold_in(key_of[12], 71), 0)
    routes_keys = jax.random.split(jax.random.fold_in(key_of[2], 1), TOKENS // TOK_DEV)
    routes_turns = jax.random.permutation(jax.random.fold_in(key_of[2], 3), TOKENS // TOK_DEV)
    routes = jax.vmap(lambda own, number: deal_out(jax.random.fold_in(key_of[2], 2), own, number, TOK_DEV, EXPERTS, TOPK, SEND, 1))(routes_keys, routes_turns).reshape((TOKENS, TOPK))
    qkv_weight = noise(key_of[3], (QKW, D), D ** -0.5, 0.15625, ((0, 8),))
    out_weight = noise(key_of[4], (D, QW), (QW // 64) ** -0.5, 1.25, ((0, 8),))
    router_weight = noise(key_of[5], (EXPERTS, D), (4 * D) ** -0.5, 0.078125, ((0, 8),))
    norm1_gain = jnp.clip(1.0 + 0.15 * jax.random.normal(key_of[6], (D,), jnp.float32), 0.25, 1.75).astype(jnp.bfloat16)
    norm2_gain = jnp.clip(1.0 + 0.15 * jax.random.normal(key_of[7], (D,), jnp.float32), 0.25, 1.75).astype(jnp.bfloat16)
    w_gate = noise(key_of[8], (EXPERTS, FFE, D), D ** -0.5, 0.15625, ((0, 8),))
    w_up = noise(key_of[9], (EXPERTS, FFE, D), D ** -0.5, 0.15625, ((0, 8),))
    w_down = noise(key_of[10], (EXPERTS, FFE, D), (FFE // 16) ** -0.5, 1.0, ((0, 8),))
    out_cotangent = noise(key_of[11], (TOKENS, D), 1.0, 6.0, ((0, 32),))
    return {"layer_in": layer_in, "segments": segments, "routes": routes, "qkv_weight": qkv_weight, "out_weight": out_weight, "router_weight": router_weight, "norm1_gain": norm1_gain, "norm2_gain": norm2_gain, "w_gate": w_gate, "w_up": w_up, "w_down": w_down, "out_cotangent": out_cotangent}


@jax.custom_vjp
def reduced_copy(v):
    return lax.optimization_barrier(v.astype(jnp.bfloat16)).astype(jnp.float32)

@jax.custom_vjp
def low_back(v):
    return v

def low_keep(v):
    return (reduced_copy(v), None)

def low_pass(kept, grad):
    return (grad,)

def back_keep(v):
    return (v, None)

def back_low(kept, grad):
    return (reduced_copy(grad),)
reduced_copy.defvjp(low_keep, low_pass)
low_back.defvjp(back_keep, back_low)
eps = 1e-06
theta = 10000.0
highest = lax.Precision.HIGHEST

def norm(hidden, gain):
    scale = lax.rsqrt(lax.optimization_barrier(jnp.mean(hidden * hidden, axis=-1, keepdims=True)) + eps)
    return hidden * scale * gain

def rotary_embed(value_matrix, token_positions):
    half = HEAD_DIMENSION // 2
    freq = theta ** (-jnp.arange(half, dtype=jnp.float32) * 2.0 / HEAD_DIMENSION)
    angle = token_positions.astype(jnp.float32)[:, None] * freq[None, :]
    cosine_table = jnp.cos(angle)[:, None, :]
    sine_table = jnp.sin(angle)[:, None, :]
    leading_entry = value_matrix[..., :half]
    second = value_matrix[..., half:]
    return jnp.concatenate([leading_entry * cosine_table - second * sine_table, second * cosine_table + leading_entry * sine_table], axis=-1)

def sequence(rows_in, segs, picks, qkv_w, out_w, router_w, gain_one, gain_two, gate_w, up_w, down_w):
    query_span_width = QUERY_HEADS * HEAD_DIMENSION
    key_span_width = KEY_VALUE_HEADS * HEAD_DIMENSION
    head_group = QUERY_HEADS // KEY_VALUE_HEADS
    token_positions = jnp.arange(SEQUENCE_TOKENS, dtype=jnp.int32)
    x_low = reduced_copy(norm(rows_in, gain_one))
    projected_rows = low_back(jnp.dot(x_low, qkv_w.T, precision=highest, preferred_element_type=jnp.float32))
    query_matrix = reduced_copy(rotary_embed(projected_rows[:, :query_span_width].reshape(SEQUENCE_TOKENS, QUERY_HEADS, HEAD_DIMENSION), token_positions)).reshape(SEQUENCE_TOKENS, KEY_VALUE_HEADS, head_group, HEAD_DIMENSION)
    key_matrix = reduced_copy(rotary_embed(projected_rows[:, query_span_width:query_span_width + key_span_width].reshape(SEQUENCE_TOKENS, KEY_VALUE_HEADS, HEAD_DIMENSION), token_positions))
    value_matrix = reduced_copy(projected_rows[:, query_span_width + key_span_width:].reshape(SEQUENCE_TOKENS, KEY_VALUE_HEADS, HEAD_DIMENSION))
    tile_block = math.gcd(SEQUENCE_TOKENS, 512)

    def attend(index):
        leading_entry = index * tile_block
        query_rows = lax.dynamic_slice_in_dim(query_matrix, leading_entry, tile_block, 0)
        query_pos = leading_entry + jnp.arange(tile_block, dtype=jnp.int32)
        query_seg = lax.dynamic_slice_in_dim(segs, leading_entry, tile_block, 0)
        score = jnp.einsum('qhgd,khd->hgqk', query_rows, key_matrix, precision=highest) * HEAD_DIMENSION ** (-0.5)
        score = low_back(score)
        valid = (query_seg[:, None] == segs[None, :]) & (token_positions[None, :] <= query_pos[:, None])
        score = jnp.where(valid, score, -1e+30)
        top = lax.optimization_barrier(jnp.max(score, axis=-1, keepdims=True))
        weight = jnp.exp(score - top)
        prob = weight / lax.optimization_barrier(jnp.sum(weight, axis=-1, keepdims=True))
        result = jnp.einsum('hgqk,khd->qhgd', reduced_copy(prob), value_matrix, precision=highest)
        return result.reshape(tile_block, query_span_width)
    attn = lax.map(jax.checkpoint(attend), jnp.arange(SEQUENCE_TOKENS // tile_block, dtype=jnp.int32)).reshape(SEQUENCE_TOKENS, query_span_width)
    mixed = reduced_copy(low_back(attn))
    branch = low_back(jnp.dot(mixed, out_w.T, precision=highest, preferred_element_type=jnp.float32))
    hidden_one = rows_in + branch
    x_two = reduced_copy(norm(hidden_one, gain_two))
    logits = low_back(jnp.dot(x_two, router_w.T, precision=highest, preferred_element_type=jnp.float32))
    chosen = jnp.take_along_axis(logits, picks, axis=1)
    gates = jax.nn.softmax(chosen, axis=-1)
    pairs = SEQUENCE_TOKENS * TOPK
    pair_expert = picks.reshape(pairs)
    marks = (pair_expert[:, None] == jnp.arange(EXPERTS, dtype=jnp.int32)[None, :]).astype(jnp.int32)
    before = jnp.cumsum(marks, axis=0, dtype=jnp.int32) - marks
    rank = lax.optimization_barrier(jnp.sum(before * marks, axis=1, dtype=jnp.int32))
    kept = rank < CAP
    dest = jnp.where(kept, pair_expert * CAP + rank, EXPERTS * CAP).astype(jnp.int32)
    owner = jnp.full((EXPERTS * CAP + 1,), pairs, jnp.int32).at[dest].set(jnp.arange(pairs, dtype=jnp.int32))[:-1]
    live = owner < pairs
    token_of = jnp.minimum(owner, pairs - 1) // TOPK
    expert_in = jnp.where(live[:, None], x_two[token_of], 0.0)
    expert_in = low_back(expert_in).reshape(EXPERTS, CAP, D)
    gate_pre = low_back(jnp.einsum('ecd,efd->ecf', expert_in, gate_w, precision=highest))
    up_pre = low_back(jnp.einsum('ecd,efd->ecf', expert_in, up_w, precision=highest))
    inner = reduced_copy(jax.nn.silu(gate_pre) * up_pre)
    expert_out = reduced_copy(low_back(jnp.einsum('ecf,efd->ecd', inner, down_w, precision=highest)))
    flat_out = jnp.concatenate([expert_out.reshape(EXPERTS * CAP, D), jnp.zeros((1, D), expert_out.dtype)], axis=0)
    pair_out = flat_out[dest].reshape(SEQUENCE_TOKENS, TOPK, D)
    return hidden_one + lax.optimization_barrier(jnp.sum(gates[:, :, None] * pair_out, axis=1))

def forward(rows_in, qkv_w, out_w, router_w, gain_one, gain_two, gate_w, up_w, down_w, segments, routes):

    def one(item):
        return sequence(item[0], item[1], item[2], qkv_w, out_w, router_w, gain_one, gain_two, gate_w, up_w, down_w)
    items = (rows_in.reshape(SEQS, SEQUENCE_TOKENS, D), segments.reshape(SEQS, SEQUENCE_TOKENS), routes.reshape(SEQS, SEQUENCE_TOKENS, TOPK))
    return lax.map(jax.checkpoint(one), items).reshape(SEQS * SEQUENCE_TOKENS, D)

def reference(layer_in, segments, routes, qkv_weight, out_weight, router_weight, norm1_gain, norm2_gain, w_gate, w_up, w_down, out_cotangent):
    primals = (layer_in.astype(jnp.float32), qkv_weight.astype(jnp.float32), out_weight.astype(jnp.float32), router_weight.astype(jnp.float32), norm1_gain.astype(jnp.float32), norm2_gain.astype(jnp.float32), w_gate.astype(jnp.float32), w_up.astype(jnp.float32), w_down.astype(jnp.float32))

    def wrapped(*value_matrix):
        return forward(*value_matrix, segments, routes)
    result, pull = jax.vjp(wrapped, *primals)
    grads = pull(out_cotangent.astype(jnp.float32))
    return (result.astype(jnp.bfloat16), grads[0].astype(jnp.bfloat16), grads[1], grads[2], grads[3], grads[4], grads[5], grads[6], grads[7], grads[8])
```

```python
import jax
import jax.numpy as jnp
from jax import lax
from jax.sharding import PartitionSpec as P

QUERY_HEADS = 24
KEY_VALUE_HEADS = 8
HEAD_DIMENSION = 64
TOPK = 8

eps = 1e-06
theta = 10000.0
negative_large = -1e30
f32 = jnp.float32
bf16 = jnp.bfloat16


def angles(token_positions, head_size):
    half = head_size // 2
    freq = theta ** (-jnp.arange(half, dtype=f32) * 2.0 / head_size)
    angle = token_positions.astype(f32)[:, None] * freq[None, :]
    return (jnp.cos(angle)[:, None, :], jnp.sin(angle)[:, None, :])


def rotate(value_matrix, cosine_table, sine_table):
    half = value_matrix.shape[-1] // 2
    first = value_matrix[..., :half]
    second = value_matrix[..., half:]
    return jnp.concatenate(
        [
            first * cosine_table - second * sine_table,
            second * cosine_table + first * sine_table,
        ],
        axis=-1,
    )


def norm_back(delta, normed, scale, gain):
    scaled = delta * gain
    return scale * (scaled - normed * jnp.mean(scaled * normed, axis=-1, keepdims=True))


def head_plan(devices):
    per_query = QUERY_HEADS // devices
    per_key = KEY_VALUE_HEADS // devices
    blocks = QUERY_HEADS + 2 * KEY_VALUE_HEADS
    own = blocks // devices

    def place(block):
        if block < QUERY_HEADS:
            return block // per_query, block % per_query
        block -= QUERY_HEADS
        if block < KEY_VALUE_HEADS:
            return block // per_key, per_query + block % per_key
        block -= KEY_VALUE_HEADS
        return block // per_key, per_query + per_key + block % per_key

    left = [[(s, *place(i * own + s)) for s in range(own)] for i in range(devices)]
    rounds = []
    for _ in range(own):
        taken = {}

        def assign(i, seen):
            for edge in left[i]:
                j = edge[1]
                if j in seen:
                    continue
                seen.add(j)
                if j not in taken or assign(taken[j][0], seen):
                    taken[j] = (i, edge)
                    return True
            return False

        for i in range(devices):
            assign(i, set())
        source_slot, target, target_slot = [0] * devices, [0] * devices, [0] * devices
        for j, (i, edge) in taken.items():
            source_slot[i], target[i], target_slot[j] = edge[0], j, edge[2]
            left[i].remove(edge)
        rounds.append((source_slot, target, target_slot))
    return rounds


def move_blocks(blocks, pick, pairs, order):
    got = [
        lax.ppermute(lax.dynamic_index_in_dim(blocks, slot, 0, keepdims=False), "ep", pair)
        for slot, pair in zip(pick, pairs)
    ]
    return jnp.stack(got)[order]


def local(
    layer_in,
    segments,
    routes,
    qkv_weight,
    out_weight,
    router_weight,
    norm1_gain,
    norm2_gain,
    w_gate,
    w_up,
    w_down,
    out_cotangent,
):
    tokens, width = layer_in.shape
    devices = lax.axis_size("ep")
    me = lax.axis_index("ep")
    copies = lax.axis_size("grp")
    mine = w_gate.shape[0]
    hidden = w_gate.shape[1]
    experts = mine * devices
    seq = tokens * devices
    capacity = 9 * tokens * TOPK // (8 * mine)
    heads = QUERY_HEADS // devices
    keys = KEY_VALUE_HEADS // devices
    group = heads // keys
    hd = HEAD_DIMENSION
    scale = hd ** (-0.5)

    x_all = lax.all_gather(layer_in, "ep", axis=0, tiled=True)
    gain_width = norm1_gain.shape[0]
    small = jnp.concatenate(
        [
            router_weight.reshape(-1),
            norm1_gain,
            norm2_gain,
            routes.T.astype(bf16).reshape(-1),
            segments.astype(bf16),
        ]
    )
    small_all = lax.all_gather(small, "ep", axis=0, tiled=False)
    cut = mine * width
    full_router = small_all[:, :cut].reshape(experts, width)
    gain_one = small_all[:, cut : cut + gain_width].reshape(1, width).astype(f32)
    gain_two = small_all[:, cut + gain_width : cut + 2 * gain_width].reshape(1, width).astype(f32)
    cut += 2 * gain_width
    routes_all = small_all[:, cut : cut + tokens * TOPK].reshape(devices, TOPK, tokens)
    routes_all = routes_all.transpose(1, 0, 2).reshape(TOPK, seq).astype(jnp.int32)
    seg_all = small_all[:, cut + tokens * TOPK :].reshape(seq)

    rounds = head_plan(devices)
    slots = len(rounds)
    to_heads = [[(i, t[i]) for i in range(devices)] for _, t, _ in rounds]
    to_rows = [[(b, a) for a, b in pair] for pair in to_heads]
    pick_row = [jnp.array(s, jnp.int32)[me] for s, _, _ in rounds]
    pick_head = [jnp.array(s, jnp.int32)[me] for _, _, s in rounds]
    order_head = jnp.array(
        [[[r[2][d] for r in rounds].index(s) for s in range(slots)] for d in range(devices)],
        jnp.int32,
    )[me]
    order_row = jnp.array(
        [[[r[0][d] for r in rounds].index(s) for s in range(slots)] for d in range(devices)],
        jnp.int32,
    )[me]
    block_rows = qkv_weight.shape[0] // slots
    qkv_heads = move_blocks(
        qkv_weight.reshape(slots, block_rows, width), pick_row, to_heads, order_head
    ).reshape(slots * block_rows, width)
    full_out = lax.all_gather(out_weight, "ep", axis=0, tiled=True)

    expert_row = jnp.arange(experts, dtype=jnp.int32)[:, None, None]
    chosen = jnp.any(routes_all[None] == expert_row, axis=1)
    own_chosen = lax.dynamic_slice_in_dim(chosen, me * mine, mine, 0)
    before = (
        jnp.arange(seq, dtype=jnp.int32)[:, None] < jnp.arange(seq, dtype=jnp.int32)[None, :]
    ).astype(bf16)
    rank = jnp.einsum(
        "es,st->et", own_chosen.astype(bf16), before, preferred_element_type=f32
    ).astype(jnp.int32)
    rank = jnp.where(own_chosen, rank, -1)
    places = jnp.arange(capacity, dtype=jnp.int32)[None, :, None]
    pick = rank[:, None, :] == places
    pick_low = pick.astype(bf16).reshape(mine * capacity, seq)

    residual_all = x_all.astype(f32)
    scale_one_all = lax.rsqrt(jnp.mean(residual_all * residual_all, axis=-1, keepdims=True) + eps)
    normed_all = residual_all * scale_one_all
    x_low = (normed_all * gain_one).astype(bf16)
    projected = jnp.einsum("td,cd->tc", x_low, qkv_heads, preferred_element_type=f32)
    positions = jnp.arange(seq, dtype=jnp.int32)
    cosine_table, sine_table = angles(positions, hd)
    turned = rotate(
        projected[:, : (heads + keys) * hd].reshape(seq, heads + keys, hd),
        cosine_table,
        sine_table,
    ).astype(bf16)
    query = turned[:, :heads].reshape(seq, keys, group, hd).transpose(1, 2, 0, 3)
    key = turned[:, heads:].transpose(1, 0, 2)
    value = (
        projected[:, (heads + keys) * hd :].astype(bf16).reshape(seq, keys, hd).transpose(1, 0, 2)
    )
    valid = (seg_all[:, None] == seg_all[None, :]) & (positions[None, :] <= positions[:, None])
    score = jnp.einsum("hgqd,hkd->hgqk", query, key, preferred_element_type=f32) * scale
    score = jnp.where(valid, score, negative_large)
    top = jnp.max(score, axis=-1, keepdims=True)
    weight = jnp.where(valid, jnp.exp(score - top), 0.0)
    prob = weight / jnp.sum(weight, axis=-1, keepdims=True)
    prob_low = prob.astype(bf16)
    attended = jnp.einsum("hgqk,hkd->hgqd", prob_low, value, preferred_element_type=f32)
    mixed_heads = attended.transpose(2, 0, 1, 3).reshape(seq, heads * hd).astype(bf16)
    mixed = lax.all_to_all(mixed_heads, "ep", split_axis=0, concat_axis=1, tiled=True)

    branch = jnp.einsum("tc,dc->td", mixed, full_out, preferred_element_type=f32)
    hidden_one = layer_in.astype(f32) + branch
    scale_two = lax.rsqrt(jnp.mean(hidden_one * hidden_one, axis=-1, keepdims=True) + eps)
    normed_two = hidden_one * scale_two
    x_two = (normed_two * gain_two).astype(bf16)
    x_two_all = lax.all_gather(x_two, "ep", axis=0, tiled=True)
    late_cotangent, late_mixed, _ = lax.optimization_barrier((out_cotangent, mixed, x_two))
    g_all = lax.all_gather(late_cotangent, "ep", axis=0, tiled=True)
    mixed_all = lax.all_gather(late_mixed, "ep", axis=0, tiled=True)

    logits = jnp.einsum("ed,td->et", full_router, x_two_all, preferred_element_type=f32)
    logits = jnp.where(chosen, logits, negative_large)
    raised = jnp.where(chosen, jnp.exp(logits - jnp.max(logits, axis=0, keepdims=True)), 0.0)
    gates = raised / jnp.sum(raised, axis=0, keepdims=True)
    own_gates = lax.dynamic_slice_in_dim(gates, me * mine, mine, 0)
    place_gate = jnp.sum(jnp.where(pick, own_gates[:, None, :], 0.0), axis=-1)[:, :, None]

    def gather(rows):
        picked = jnp.einsum("pt,td->pd", pick_low, rows, preferred_element_type=f32)
        return picked.astype(bf16).reshape(mine, capacity, width)

    def scatter(rows):
        back = jnp.einsum(
            "pt,pd->td", pick_low, rows.reshape(mine * capacity, width), preferred_element_type=f32
        )
        return back.astype(bf16)

    def shares(left, right):
        grad = jnp.einsum("jcf,jcd->jfd", left, right, preferred_element_type=f32).astype(bf16)
        grad = grad.reshape(mine * hidden, copies, width // copies).transpose(1, 0, 2)
        return grad.reshape(copies * mine * hidden, width // copies)

    def grp_sum(part):
        total = lax.psum_scatter(part, "grp", scatter_dimension=0, tiled=True)
        return total.astype(f32).reshape(mine, hidden, width // copies)

    dense_in = gather(x_two_all)
    dense_g = gather(g_all)
    gate_pre = jnp.einsum("jcd,jfd->jcf", dense_in, w_gate, preferred_element_type=f32)
    up_pre = jnp.einsum("jcd,jfd->jcf", dense_in, w_up, preferred_element_type=f32)
    logistic = jax.nn.sigmoid(gate_pre)
    inner = (gate_pre * logistic * up_pre).astype(bf16)
    expert_out = jnp.einsum("jcf,jfd->jcd", inner, w_down, preferred_element_type=f32)
    place_dgate = jnp.sum(expert_out * dense_g.astype(f32), axis=-1)
    dgate_own = jnp.sum(jnp.where(pick, place_dgate[:, :, None], 0.0), axis=1)
    out_part = scatter((place_gate * expert_out).astype(bf16))
    dense_grad = (place_gate * dense_g.astype(f32)).astype(bf16)
    inner_grad = jnp.einsum("jcd,jfd->jcf", dense_grad, w_down, preferred_element_type=f32)
    gate_back = (inner_grad * up_pre * logistic * (1.0 + gate_pre * (1.0 - logistic))).astype(bf16)
    up_back = (inner_grad * gate_pre * logistic).astype(bf16)
    slot_grad = jnp.einsum(
        "jcf,jfd->jcd", gate_back, w_gate, preferred_element_type=f32
    ) + jnp.einsum("jcf,jfd->jcd", up_back, w_up, preferred_element_type=f32)
    back_part = scatter(slot_grad.astype(bf16))
    two_grad = lax.psum_scatter(back_part, "ep", scatter_dimension=0, tiled=True).astype(f32)
    dgate = lax.all_to_all(dgate_own, "ep", split_axis=1, concat_axis=0, tiled=True)
    down_part = shares(inner, dense_grad)
    gate_part = shares(gate_back, dense_in)
    up_part = shares(up_back, dense_in)

    delta = out_cotangent.astype(f32)
    gates_here = lax.dynamic_slice_in_dim(gates, me * tokens, tokens, 1)
    chosen_grad = gates_here * (dgate - jnp.sum(gates_here * dgate, axis=0, keepdims=True))
    logit_grad = chosen_grad.astype(bf16)
    router_grad = jnp.einsum("et,td->ed", logit_grad, x_two, preferred_element_type=f32)
    two_grad = two_grad + jnp.einsum(
        "et,ed->td", logit_grad, full_router, preferred_element_type=f32
    )
    gain_two_grad = jnp.sum(two_grad * normed_two, axis=0, keepdims=True)
    hidden_grad = delta + norm_back(two_grad, normed_two, scale_two, gain_two)
    hidden_low = hidden_grad.astype(bf16)
    mixing = jnp.einsum("td,dc->tc", hidden_low, full_out, preferred_element_type=f32)
    mixing_heads = lax.all_to_all(
        mixing.astype(bf16), "ep", split_axis=1, concat_axis=0, tiled=True
    )
    hidden_cols = lax.all_to_all(hidden_low, "ep", split_axis=1, concat_axis=0, tiled=True)

    change = mixing_heads.reshape(seq, keys, group, hd).transpose(1, 2, 0, 3)
    prob_grad = jnp.einsum("hgqd,hkd->hgqk", change, value, preferred_element_type=f32)
    row = jnp.sum(prob * prob_grad, axis=-1, keepdims=True)
    score_grad = (prob * (prob_grad - row)).astype(bf16)
    value_grad = jnp.einsum("hgqk,hgqd->hkd", prob_low, change, preferred_element_type=f32)
    query_grad = jnp.einsum("hgqk,hkd->hgqd", score_grad, key, preferred_element_type=f32) * scale
    key_grad = jnp.einsum("hgqk,hgqd->hkd", score_grad, query, preferred_element_type=f32) * scale
    turned_grad = jnp.concatenate(
        [
            query_grad.transpose(2, 0, 1, 3).reshape(seq, heads, hd),
            key_grad.transpose(1, 0, 2),
        ],
        axis=1,
    )
    turned_grad = rotate(turned_grad, cosine_table, -sine_table).reshape(seq, (heads + keys) * hd)
    proj_grad = jnp.concatenate(
        [turned_grad, value_grad.transpose(1, 0, 2).reshape(seq, keys * hd)], axis=1
    ).astype(bf16)
    one_part = jnp.einsum("tc,cd->td", proj_grad, qkv_heads, preferred_element_type=f32)
    gain_one_grad = jnp.sum(one_part * normed_all, axis=0, keepdims=True)
    one_grad = lax.psum_scatter(
        one_part.astype(bf16), "ep", scatter_dimension=0, tiled=True
    ).astype(f32)
    qkv_grad = jnp.einsum("tc,td->cd", proj_grad, x_low, preferred_element_type=f32)
    out_grad = jnp.einsum("td,tc->dc", hidden_cols, mixed_all, preferred_element_type=f32)

    small_sum = lax.psum(
        jnp.concatenate([router_grad, gain_one_grad, gain_two_grad], axis=0), ("grp", "ep")
    )
    router_sum = lax.dynamic_slice_in_dim(small_sum[:experts], me * mine, mine, 0)
    gain_sums = lax.dynamic_slice_in_dim(small_sum[experts:], me * gain_width, gain_width, 1)
    qkv_sum = lax.psum(qkv_grad.astype(bf16), "grp")
    qkv_rows = move_blocks(
        qkv_sum.reshape(slots, block_rows, width), pick_head, to_rows, order_row
    ).reshape(slots * block_rows, width)
    out_sum = lax.psum(out_grad.astype(bf16), "grp")

    returned = lax.psum_scatter(out_part, "ep", scatter_dimension=0, tiled=True)
    layer_out = (hidden_one + returned.astype(f32)).astype(bf16)
    residual = layer_in.astype(f32)
    scale_one = lax.rsqrt(jnp.mean(residual * residual, axis=-1, keepdims=True) + eps)
    grad_in = (hidden_grad + norm_back(one_grad, residual * scale_one, scale_one, gain_one)).astype(
        bf16
    )
    return (
        layer_out,
        grad_in,
        qkv_rows.astype(f32),
        out_sum.astype(f32),
        router_sum,
        gain_sums[0],
        gain_sums[1],
        grp_sum(gate_part),
        grp_sum(up_part),
        grp_sum(down_part),
    )


def solution(mesh):
    in_specs = (
        P(("grp", "ep"), None),
        P(("grp", "ep")),
        P(("grp", "ep"), None),
        P("ep", None),
        P("ep", None),
        P("ep", None),
        P("ep"),
        P("ep"),
        P("ep", None, None),
        P("ep", None, None),
        P("ep", None, None),
        P(("grp", "ep"), None),
    )
    out_specs = (
        P(("grp", "ep"), None),
        P(("grp", "ep"), None),
        P("ep", None),
        P("ep", None),
        P("ep", None),
        P("ep"),
        P("ep"),
        P("ep", None, "grp"),
        P("ep", None, "grp"),
        P("ep", None, "grp"),
    )
    return jax.shard_map(local, mesh=mesh, in_specs=in_specs, out_specs=out_specs, check_vma=False)
```

```python
import jax
import jax.numpy as jnp
from jax import lax
from jax.sharding import PartitionSpec as P

QUERY_HEADS = 24
KEY_VALUE_HEADS = 8
HEAD_DIMENSION = 64
TOPK = 8

eps = 1e-06
theta = 10000.0
negative_large = -1e30
f32 = jnp.float32
bf16 = jnp.bfloat16


def angles(token_positions, head_size):
    half = head_size // 2
    freq = theta ** (-jnp.arange(half, dtype=f32) * 2.0 / head_size)
    angle = token_positions.astype(f32)[:, None] * freq[None, :]
    return (jnp.cos(angle)[:, None, :], jnp.sin(angle)[:, None, :])


def rotate(value_matrix, cosine_table, sine_table):
    half = value_matrix.shape[-1] // 2
    first = value_matrix[..., :half]
    second = value_matrix[..., half:]
    return jnp.concatenate(
        [
            first * cosine_table - second * sine_table,
            second * cosine_table + first * sine_table,
        ],
        axis=-1,
    )


def norm_back(delta, normed, scale, gain):
    scaled = delta * gain
    return scale * (scaled - normed * jnp.mean(scaled * normed, axis=-1, keepdims=True))


def head_plan(devices):
    per_query = QUERY_HEADS // devices
    per_key = KEY_VALUE_HEADS // devices
    blocks = QUERY_HEADS + 2 * KEY_VALUE_HEADS
    own = blocks // devices

    def place(block):
        if block < QUERY_HEADS:
            return block // per_query, block % per_query
        block -= QUERY_HEADS
        if block < KEY_VALUE_HEADS:
            return block // per_key, per_query + block % per_key
        block -= KEY_VALUE_HEADS
        return block // per_key, per_query + per_key + block % per_key

    left = [[(s, *place(i * own + s)) for s in range(own)] for i in range(devices)]
    rounds = []
    for _ in range(own):
        taken = {}

        def assign(i, seen):
            for edge in left[i]:
                j = edge[1]
                if j in seen:
                    continue
                seen.add(j)
                if j not in taken or assign(taken[j][0], seen):
                    taken[j] = (i, edge)
                    return True
            return False

        for i in range(devices):
            assign(i, set())
        source_slot, target, target_slot = [0] * devices, [0] * devices, [0] * devices
        for j, (i, edge) in taken.items():
            source_slot[i], target[i], target_slot[j] = edge[0], j, edge[2]
            left[i].remove(edge)
        rounds.append((source_slot, target, target_slot))
    return rounds


def move_blocks(blocks, pick, pairs, order):
    got = [
        lax.ppermute(lax.dynamic_index_in_dim(blocks, slot, 0, keepdims=False), "ep", pair)
        for slot, pair in zip(pick, pairs)
    ]
    return jnp.stack(got)[order]


def grp_direct(copies):
    return copies in (2, 4)


def grp_send(value, step, copies):
    return lax.ppermute(value, "grp", [(a, a ^ step) for a in range(copies)])


def grp_gather(block, copies, at):
    if not grp_direct(copies):
        return lax.all_gather(block, "grp", axis=0, tiled=False)
    got = jnp.stack([block] + [grp_send(block, d, copies) for d in range(1, copies)])
    return got[jnp.arange(copies, dtype=jnp.int32) ^ at]


def grp_total(value, copies):
    if not grp_direct(copies):
        return lax.psum(value, "grp")
    return value + sum(grp_send(value, d, copies) for d in range(1, copies))


def grp_all_sum(rows, copies, at):
    if not grp_direct(copies):
        return lax.psum(rows, "grp").astype(f32)
    blocks = rows.reshape(copies, rows.shape[0] // copies, rows.shape[1])
    total = lax.dynamic_index_in_dim(blocks, at, 0, keepdims=False).astype(f32)
    for d in range(1, copies):
        part = lax.dynamic_index_in_dim(blocks, at ^ d, 0, keepdims=False)
        total = total + grp_send(part, d, copies).astype(f32)
    return grp_gather(total.astype(bf16), copies, at).reshape(rows.shape).astype(f32)


def local(
    layer_in,
    segments,
    routes,
    qkv_weight,
    out_weight,
    router_weight,
    norm1_gain,
    norm2_gain,
    w_gate,
    w_up,
    w_down,
    out_cotangent,
):
    tokens, width = layer_in.shape
    devices = lax.axis_size("ep")
    me = lax.axis_index("ep")
    copies = lax.axis_size("grp")
    at = lax.axis_index("grp")
    mine = w_gate.shape[0]
    hidden = w_gate.shape[1]
    experts = mine * devices
    seq = tokens * devices
    capacity = 9 * tokens * TOPK // (8 * mine)
    heads = QUERY_HEADS // devices
    keys = KEY_VALUE_HEADS // devices
    group = heads // keys
    hd = HEAD_DIMENSION
    scale = hd ** (-0.5)

    x_all = lax.all_gather(layer_in, "ep", axis=0, tiled=True)
    gain_width = norm1_gain.shape[0]
    small = jnp.concatenate(
        [
            router_weight.reshape(-1),
            norm1_gain,
            norm2_gain,
            routes.T.astype(bf16).reshape(-1),
            segments.astype(bf16),
        ]
    )
    small_all = lax.all_gather(small, "ep", axis=0, tiled=False)
    cut = mine * width
    full_router = small_all[:, :cut].reshape(experts, width)
    gain_one = small_all[:, cut : cut + gain_width].reshape(1, width).astype(f32)
    gain_two = small_all[:, cut + gain_width : cut + 2 * gain_width].reshape(1, width).astype(f32)
    cut += 2 * gain_width
    routes_all = small_all[:, cut : cut + tokens * TOPK].reshape(devices, TOPK, tokens)
    routes_all = routes_all.transpose(1, 0, 2).reshape(TOPK, seq).astype(jnp.int32)
    seg_all = small_all[:, cut + tokens * TOPK :].reshape(seq)

    rounds = head_plan(devices)
    slots = len(rounds)
    to_heads = [[(i, t[i]) for i in range(devices)] for _, t, _ in rounds]
    to_rows = [[(b, a) for a, b in pair] for pair in to_heads]
    pick_row = [jnp.array(s, jnp.int32)[me] for s, _, _ in rounds]
    pick_head = [jnp.array(s, jnp.int32)[me] for _, _, s in rounds]
    order_head = jnp.array(
        [[[r[2][d] for r in rounds].index(s) for s in range(slots)] for d in range(devices)],
        jnp.int32,
    )[me]
    order_row = jnp.array(
        [[[r[0][d] for r in rounds].index(s) for s in range(slots)] for d in range(devices)],
        jnp.int32,
    )[me]
    block_rows = qkv_weight.shape[0] // slots
    late_qkv, _ = lax.optimization_barrier((qkv_weight, small_all))
    qkv_heads = move_blocks(
        late_qkv.reshape(slots, block_rows, width), pick_row, to_heads, order_head
    ).reshape(slots * block_rows, width)
    if grp_direct(copies):
        out_rows = out_weight.reshape(copies, -1, width)
        out_quarter = lax.all_gather(
            lax.dynamic_index_in_dim(out_rows, at, 0, keepdims=False), "ep", axis=0, tiled=False
        )
        full_out = grp_gather(out_quarter, copies, at)
        full_out = full_out.transpose(1, 0, 2, 3).reshape(-1, width)
    else:
        full_out = lax.all_gather(out_weight, "ep", axis=0, tiled=True)

    late_cotangent, _ = lax.optimization_barrier((out_cotangent, x_all))
    g_all = lax.all_gather(late_cotangent, "ep", axis=0, tiled=True)

    expert_row = jnp.arange(experts, dtype=jnp.int32)[:, None, None]
    chosen = jnp.any(routes_all[None] == expert_row, axis=1)
    own_chosen = lax.dynamic_slice_in_dim(chosen, me * mine, mine, 0)
    before = (
        jnp.arange(seq, dtype=jnp.int32)[:, None] < jnp.arange(seq, dtype=jnp.int32)[None, :]
    ).astype(bf16)
    rank = jnp.einsum(
        "es,st->et", own_chosen.astype(bf16), before, preferred_element_type=f32
    ).astype(jnp.int32)
    rank = jnp.where(own_chosen, rank, -1)
    places = jnp.arange(capacity, dtype=jnp.int32)[None, :, None]
    pick = rank[:, None, :] == places
    pick_low = pick.astype(bf16).reshape(mine * capacity, seq)
    pick_back = (rank.T[:, :, None] == jnp.arange(capacity, dtype=jnp.int32)[None, None, :]).astype(
        bf16
    )
    pick_back = pick_back.reshape(seq, mine * capacity)

    residual_all = x_all.astype(f32)
    scale_one_all = lax.rsqrt(jnp.mean(residual_all * residual_all, axis=-1, keepdims=True) + eps)
    normed_all = residual_all * scale_one_all
    x_low = (normed_all * gain_one).astype(bf16)
    projected = jnp.einsum("td,cd->tc", x_low, qkv_heads, preferred_element_type=f32)
    positions = jnp.arange(seq, dtype=jnp.int32)
    cosine_table, sine_table = angles(positions, hd)
    turned = rotate(
        projected[:, : (heads + keys) * hd].reshape(seq, heads + keys, hd),
        cosine_table,
        sine_table,
    ).astype(bf16)
    query = turned[:, :heads].reshape(seq, keys, group, hd).transpose(1, 2, 0, 3)
    key = turned[:, heads:].transpose(1, 0, 2)
    value = (
        projected[:, (heads + keys) * hd :].astype(bf16).reshape(seq, keys, hd).transpose(1, 0, 2)
    )
    valid = (seg_all[:, None] == seg_all[None, :]) & (positions[None, :] <= positions[:, None])
    score = jnp.einsum("hgqd,hkd->hgqk", query, key, preferred_element_type=f32) * scale
    score = jnp.where(valid, score, negative_large)
    top = jnp.max(score, axis=-1, keepdims=True)
    weight = jnp.where(valid, jnp.exp(score - top), 0.0)
    prob = weight / jnp.sum(weight, axis=-1, keepdims=True)
    prob_low = prob.astype(bf16)
    attended = jnp.einsum("hgqk,hkd->hgqd", prob_low, value, preferred_element_type=f32)
    mixed_heads = attended.transpose(2, 0, 1, 3).reshape(seq, heads * hd).astype(bf16)
    mixed = lax.all_to_all(mixed_heads, "ep", split_axis=0, concat_axis=1, tiled=True)

    branch = jnp.einsum("tc,dc->td", mixed, full_out, preferred_element_type=f32)
    hidden_one = layer_in.astype(f32) + branch
    scale_two = lax.rsqrt(jnp.mean(hidden_one * hidden_one, axis=-1, keepdims=True) + eps)
    normed_two = hidden_one * scale_two
    x_two = (normed_two * gain_two).astype(bf16)
    x_two_all = lax.all_gather(x_two, "ep", axis=0, tiled=True)
    late_mixed, _ = lax.optimization_barrier((mixed, x_two))
    mixed_all = lax.all_gather(late_mixed, "ep", axis=0, tiled=True)

    logits = jnp.einsum("ed,td->et", full_router, x_two_all, preferred_element_type=f32)
    logits = jnp.where(chosen, logits, negative_large)
    raised = jnp.where(chosen, jnp.exp(logits - jnp.max(logits, axis=0, keepdims=True)), 0.0)
    gates = raised / jnp.sum(raised, axis=0, keepdims=True)
    own_gates = lax.dynamic_slice_in_dim(gates, me * mine, mine, 0)
    place_gate = jnp.sum(jnp.where(pick, own_gates[:, None, :], 0.0), axis=-1)[:, :, None]

    def gather(rows):
        picked = jnp.einsum("pt,td->pd", pick_low, rows, preferred_element_type=f32)
        return picked.astype(bf16).reshape(mine, capacity, width)

    def scatter(rows):
        back = jnp.einsum(
            "tp,pd->td", pick_back, rows.reshape(mine * capacity, width), preferred_element_type=f32
        )
        return back.astype(bf16)

    cols = width // copies

    def column_blocks(rows):
        if not grp_direct(copies):
            return rows
        return [
            lax.dynamic_slice_in_dim(rows, (at ^ d) * cols, cols, 2) for d in range(copies)
        ]

    def shares(left, blocks):
        if not grp_direct(copies):
            return jnp.einsum("jcf,jcd->jfd", left, blocks, preferred_element_type=f32).astype(bf16)
        parts = [
            jnp.einsum("jcf,jcd->jfd", left, block, preferred_element_type=f32) for block in blocks
        ]
        return [parts[0]] + [part.astype(bf16) for part in parts[1:]]

    def grp_sum(parts):
        if not grp_direct(copies):
            return lax.psum_scatter(parts, "grp", scatter_dimension=2, tiled=True).astype(f32)
        got = [grp_send(parts[d], d, copies).astype(f32) for d in range(1, copies)]
        return parts[0] + sum(got)

    dense_g = gather(g_all)
    x_two_all, dense_g, pick_back = lax.optimization_barrier((x_two_all, dense_g, pick_back))
    dense_in = gather(x_two_all)
    gate_pre = jnp.einsum("jcd,jfd->jcf", dense_in, w_gate, preferred_element_type=f32)
    up_pre = jnp.einsum("jcd,jfd->jcf", dense_in, w_up, preferred_element_type=f32)
    logistic = jax.nn.sigmoid(gate_pre)
    inner = (gate_pre * logistic * up_pre).astype(bf16)
    expert_out = jnp.einsum("jcf,jfd->jcd", inner, w_down, preferred_element_type=f32)
    place_dgate = jnp.sum(expert_out * dense_g.astype(f32), axis=-1)
    dgate_own = jnp.sum(jnp.where(pick, place_dgate[:, :, None], 0.0), axis=1)
    out_part = scatter((place_gate * expert_out).astype(bf16))
    dense_grad = (place_gate * dense_g.astype(f32)).astype(bf16)
    inner_grad = jnp.einsum("jcd,jfd->jcf", dense_grad, w_down, preferred_element_type=f32)
    gate_back = (inner_grad * up_pre * logistic * (1.0 + gate_pre * (1.0 - logistic))).astype(bf16)
    up_back = (inner_grad * gate_pre * logistic).astype(bf16)
    slot_grad = jnp.einsum(
        "jcf,jfd->jcd", gate_back, w_gate, preferred_element_type=f32
    ) + jnp.einsum("jcf,jfd->jcd", up_back, w_up, preferred_element_type=f32)
    back_part = scatter(slot_grad.astype(bf16))
    two_grad = lax.psum_scatter(back_part, "ep", scatter_dimension=0, tiled=True).astype(f32)
    dgate = lax.all_to_all(dgate_own, "ep", split_axis=1, concat_axis=0, tiled=True)
    in_blocks = column_blocks(dense_in)
    down_part = shares(inner, column_blocks(dense_grad))
    gate_part = shares(gate_back, in_blocks)
    up_part = shares(up_back, in_blocks)
    two_grad, out_part, down_part, gate_part, up_part = lax.optimization_barrier(
        (two_grad, out_part, down_part, gate_part, up_part)
    )
    returned = lax.psum_scatter(out_part, "ep", scatter_dimension=0, tiled=True)

    delta = out_cotangent.astype(f32)
    gates_here = lax.dynamic_slice_in_dim(gates, me * tokens, tokens, 1)
    chosen_grad = gates_here * (dgate - jnp.sum(gates_here * dgate, axis=0, keepdims=True))
    logit_grad = chosen_grad.astype(bf16)
    router_grad = jnp.einsum("et,td->ed", logit_grad, x_two, preferred_element_type=f32)
    two_grad = two_grad + jnp.einsum(
        "et,ed->td", logit_grad, full_router, preferred_element_type=f32
    )
    gain_two_grad = jnp.sum(two_grad * normed_two, axis=0, keepdims=True)
    hidden_grad = delta + norm_back(two_grad, normed_two, scale_two, gain_two)
    hidden_low = hidden_grad.astype(bf16)
    mixing = jnp.einsum("td,dc->tc", hidden_low, full_out, preferred_element_type=f32)
    mixing_heads = lax.all_to_all(
        mixing.astype(bf16), "ep", split_axis=1, concat_axis=0, tiled=True
    )
    hidden_cols = lax.all_to_all(hidden_low, "ep", split_axis=1, concat_axis=0, tiled=True)

    change = mixing_heads.reshape(seq, keys, group, hd).transpose(1, 2, 0, 3)
    prob_grad = jnp.einsum("hgqd,hkd->hgqk", change, value, preferred_element_type=f32)
    row = jnp.sum(prob * prob_grad, axis=-1, keepdims=True)
    score_grad = (prob * (prob_grad - row)).astype(bf16)
    value_grad = jnp.einsum("hgqk,hgqd->hkd", prob_low, change, preferred_element_type=f32)
    query_grad = jnp.einsum("hgqk,hkd->hgqd", score_grad, key, preferred_element_type=f32) * scale
    key_grad = jnp.einsum("hgqk,hgqd->hkd", score_grad, query, preferred_element_type=f32) * scale
    turned_grad = jnp.concatenate(
        [
            query_grad.transpose(2, 0, 1, 3).reshape(seq, heads, hd),
            key_grad.transpose(1, 0, 2),
        ],
        axis=1,
    )
    turned_grad = rotate(turned_grad, cosine_table, -sine_table).reshape(seq, (heads + keys) * hd)
    proj_grad = jnp.concatenate(
        [turned_grad, value_grad.transpose(1, 0, 2).reshape(seq, keys * hd)], axis=1
    ).astype(bf16)
    one_part = jnp.einsum("tc,cd->td", proj_grad, qkv_heads, preferred_element_type=f32)
    gain_one_grad = jnp.sum(one_part * normed_all, axis=0, keepdims=True)
    one_grad = lax.psum_scatter(
        one_part.astype(bf16), "ep", scatter_dimension=0, tiled=True
    ).astype(f32)
    proj_rows = move_blocks(
        proj_grad.T.reshape(slots, block_rows, seq), pick_head, to_rows, order_row
    ).reshape(slots * block_rows, seq)
    qkv_grad = jnp.einsum("ct,td->cd", proj_rows, x_low, preferred_element_type=f32)
    out_grad = jnp.einsum("td,tc->dc", hidden_cols, mixed_all, preferred_element_type=f32)

    gain_pack = jnp.concatenate([gain_one_grad, gain_two_grad], axis=0)
    gain_pack = gain_pack.reshape(2, devices, gain_width).transpose(1, 0, 2)
    gain_pack = gain_pack.reshape(devices, 1, 2 * gain_width)
    gain_pack = jnp.pad(gain_pack, ((0, 0), (0, 0), (0, width - 2 * gain_width)))
    small_pack = jnp.concatenate([router_grad.reshape(devices, mine, width), gain_pack], axis=1)
    small_pack = lax.all_to_all(small_pack, "ep", split_axis=0, concat_axis=0, tiled=True)
    small_sum = grp_total(jnp.sum(small_pack, axis=0), copies)
    qkv_sum = grp_all_sum(qkv_grad.astype(bf16), copies, at)
    out_sum = grp_all_sum(out_grad.astype(bf16), copies, at)

    layer_out = (hidden_one + returned.astype(f32)).astype(bf16)
    residual = layer_in.astype(f32)
    scale_one = lax.rsqrt(jnp.mean(residual * residual, axis=-1, keepdims=True) + eps)
    grad_in = (hidden_grad + norm_back(one_grad, residual * scale_one, scale_one, gain_one)).astype(
        bf16
    )
    return (
        layer_out,
        grad_in,
        qkv_sum,
        out_sum,
        small_sum[:mine],
        small_sum[mine, :gain_width],
        small_sum[mine, gain_width : 2 * gain_width],
        grp_sum(gate_part),
        grp_sum(up_part),
        grp_sum(down_part),
    )


def solution(mesh):
    in_specs = (
        P(("grp", "ep"), None),
        P(("grp", "ep")),
        P(("grp", "ep"), None),
        P("ep", None),
        P("ep", None),
        P("ep", None),
        P("ep"),
        P("ep"),
        P("ep", None, None),
        P("ep", None, None),
        P("ep", None, None),
        P(("grp", "ep"), None),
    )
    out_specs = (
        P(("grp", "ep"), None),
        P(("grp", "ep"), None),
        P("ep", None),
        P("ep", None),
        P("ep", None),
        P("ep"),
        P("ep"),
        P("ep", None, "grp"),
        P("ep", None, "grp"),
        P("ep", None, "grp"),
    )
    return jax.shard_map(local, mesh=mesh, in_specs=in_specs, out_specs=out_specs, check_vma=False)
```

```python
import jax
import jax.numpy as jnp
from jax import lax
from jax.sharding import PartitionSpec as P


QUERY_HEADS = 24
KEY_VALUE_HEADS = 8
HEAD_DIMENSION = 64
TOPK = 8


eps = 1e-06
theta = 10000.0
negative_large = -1e30
f32 = jnp.float32
bf16 = jnp.bfloat16


def angles(token_positions, head_size):
    half = head_size // 2
    freq = theta ** (-jnp.arange(half, dtype=f32) * 2.0 / head_size)
    angle = token_positions.astype(f32)[:, None] * freq[None, :]
    return (jnp.cos(angle)[:, None, :], jnp.sin(angle)[:, None, :])


def rotate(value_matrix, cosine_table, sine_table):
    half = value_matrix.shape[-1] // 2
    first = value_matrix[..., :half]
    second = value_matrix[..., half:]
    return jnp.concatenate(
        [
            first * cosine_table - second * sine_table,
            second * cosine_table + first * sine_table,
        ],
        axis=-1,
    )


def norm_back(delta, normed, scale, gain):
    scaled = delta * gain
    return scale * (scaled - normed * jnp.mean(scaled * normed, axis=-1, keepdims=True))


def head_plan(devices):
    per_query = QUERY_HEADS // devices
    per_key = KEY_VALUE_HEADS // devices
    blocks = QUERY_HEADS + 2 * KEY_VALUE_HEADS
    own = blocks // devices

    def place(block):
        if block < QUERY_HEADS:
            return block // per_query, block % per_query
        block -= QUERY_HEADS
        if block < KEY_VALUE_HEADS:
            return block // per_key, per_query + block % per_key
        block -= KEY_VALUE_HEADS
        return block // per_key, per_query + per_key + block % per_key

    left = [[(s, *place(i * own + s)) for s in range(own)] for i in range(devices)]
    rounds = []
    for _ in range(own):
        taken = {}

        def assign(i, seen):
            for edge in left[i]:
                j = edge[1]
                if j in seen:
                    continue
                seen.add(j)
                if j not in taken or assign(taken[j][0], seen):
                    taken[j] = (i, edge)
                    return True
            return False

        for i in range(devices):
            assign(i, set())
        source_slot, target, target_slot = [0] * devices, [0] * devices, [0] * devices
        for j, (i, edge) in taken.items():
            source_slot[i], target[i], target_slot[j] = edge[0], j, edge[2]
            left[i].remove(edge)
        rounds.append((source_slot, target, target_slot))
    return rounds


def move_blocks(blocks, pick, pairs, order):
    chosen = blocks[pick]
    return jnp.stack([lax.ppermute(chosen[p], "ep", pair) for p, pair in enumerate(pairs)])[order]


def grp_direct(copies):
    return copies in (2, 4)


def grp_send(value, step, copies):
    return lax.ppermute(value, "grp", [(a, a ^ step) for a in range(copies)])


def grp_gather(block, copies, at):
    if not grp_direct(copies):
        return lax.all_gather(block, "grp", axis=0, tiled=False)
    got = jnp.stack([block] + [grp_send(block, d, copies) for d in range(1, copies)])
    return got[jnp.arange(copies, dtype=jnp.int32) ^ at]


def grp_total(value, copies):
    if not grp_direct(copies):
        return lax.psum(value, "grp")
    return value + sum(grp_send(value, d, copies) for d in range(1, copies))


def grp_all_sum(rows, copies, at):
    if not grp_direct(copies):
        return lax.psum(rows, "grp").astype(f32)
    blocks = rows.reshape(copies, rows.shape[0] // copies, rows.shape[1])
    total = lax.dynamic_index_in_dim(blocks, at, 0, keepdims=False).astype(f32)
    for d in range(1, copies):
        part = lax.dynamic_index_in_dim(blocks, at ^ d, 0, keepdims=False)
        total = total + grp_send(part, d, copies).astype(f32)
    return grp_gather(total.astype(bf16), copies, at).reshape(rows.shape).astype(f32)


def local(
    layer_in,
    segments,
    routes,
    qkv_weight,
    out_weight,
    router_weight,
    norm1_gain,
    norm2_gain,
    w_gate,
    w_up,
    w_down,
    out_cotangent,
):
    tokens, width = layer_in.shape
    devices = lax.axis_size("ep")
    me = lax.axis_index("ep")
    copies = lax.axis_size("grp")
    at = lax.axis_index("grp")
    mine = w_gate.shape[0]
    hidden = w_gate.shape[1]
    experts = mine * devices
    seq = tokens * devices
    capacity = 9 * tokens * TOPK // (8 * mine)
    heads = QUERY_HEADS // devices
    keys = KEY_VALUE_HEADS // devices
    group = heads // keys
    hd = HEAD_DIMENSION
    scale = hd ** (-0.5)

    x_all = lax.all_gather(layer_in, "ep", axis=0, tiled=True)
    gain_width = norm1_gain.shape[0]
    small = jnp.concatenate(
        [
            router_weight.reshape(-1),
            norm1_gain,
            norm2_gain,
            routes.T.astype(bf16).reshape(-1),
            segments.astype(bf16),
        ]
    )
    small_all = lax.all_gather(small, "ep", axis=0, tiled=False)
    cut = mine * width
    full_router = small_all[:, :cut].reshape(experts, width)
    gain_one = small_all[:, cut : cut + gain_width].reshape(1, width).astype(f32)
    gain_two = small_all[:, cut + gain_width : cut + 2 * gain_width].reshape(1, width).astype(f32)
    cut += 2 * gain_width
    routes_all = small_all[:, cut : cut + tokens * TOPK].reshape(devices, TOPK, tokens)
    routes_all = routes_all.transpose(1, 0, 2).reshape(TOPK, seq).astype(jnp.int32)
    seg_all = small_all[:, cut + tokens * TOPK :].reshape(seq)

    rounds = head_plan(devices)
    slots = len(rounds)
    to_heads = [[(i, t[i]) for i in range(devices)] for _, t, _ in rounds]
    to_rows = [[(b, a) for a, b in pair] for pair in to_heads]
    table = []
    for d in range(devices):
        put = [[r[2][d] for r in rounds].index(s) for s in range(slots)]
        back = [[r[0][d] for r in rounds].index(s) for s in range(slots)]
        table.append([r[0][d] for r in rounds] + [r[2][d] for r in rounds] + put + back)
    row = jnp.array(table, jnp.int32)[me]
    pick_row, pick_head, order_head, order_row = (
        row[n * slots : (n + 1) * slots] for n in range(4)
    )
    block_rows = qkv_weight.shape[0] // slots
    late_qkv, _ = lax.optimization_barrier((qkv_weight, small_all))
    qkv_heads = move_blocks(
        late_qkv.reshape(slots, block_rows, width), pick_row, to_heads, order_head
    ).reshape(slots * block_rows, width)
    if grp_direct(copies):
        out_cols = out_weight.shape[1] // copies
        out_quarter = lax.dynamic_slice_in_dim(out_weight, at * out_cols, out_cols, 1)
        out_quarter = lax.all_gather(out_quarter, "ep", axis=0, tiled=True)
        out_parts = [out_quarter] + [grp_send(out_quarter, d, copies) for d in range(1, copies)]
        spans = [(at ^ d) * out_cols for d in range(copies)]
        ordered = jnp.arange(copies, dtype=jnp.int32) ^ at
    else:
        out_cols = out_weight.shape[1]
        out_parts = [lax.all_gather(out_weight, "ep", axis=0, tiled=True)]
        spans = [0]
        ordered = jnp.zeros((1,), jnp.int32)
    w_pair = jnp.concatenate([w_gate, w_up], axis=1)

    late_cotangent, _ = lax.optimization_barrier((out_cotangent, x_all))
    g_all = lax.all_gather(late_cotangent, "ep", axis=0, tiled=True)

    expert_row = jnp.arange(experts, dtype=jnp.int32)[:, None, None]
    chosen = jnp.any(routes_all[None] == expert_row, axis=1)
    own_chosen = lax.dynamic_slice_in_dim(chosen, me * mine, mine, 0)
    before = (
        jnp.arange(seq, dtype=jnp.int32)[:, None] < jnp.arange(seq, dtype=jnp.int32)[None, :]
    ).astype(bf16)
    rank = jnp.einsum(
        "es,st->et", own_chosen.astype(bf16), before, preferred_element_type=f32
    ).astype(jnp.int32)
    rank = jnp.where(own_chosen, rank, -1)
    places = jnp.arange(capacity, dtype=jnp.int32)[None, :, None]
    pick = rank[:, None, :] == places
    pick_low = pick.astype(bf16).reshape(mine * capacity, seq)
    pick_back = (rank.T[:, :, None] == jnp.arange(capacity, dtype=jnp.int32)[None, None, :]).astype(
        bf16
    )
    pick_back = pick_back.reshape(seq, mine * capacity)

    residual_all = x_all.astype(f32)
    scale_one_all = lax.rsqrt(jnp.mean(residual_all * residual_all, axis=-1, keepdims=True) + eps)
    normed_all = residual_all * scale_one_all
    x_low = (normed_all * gain_one).astype(bf16)
    projected = jnp.einsum("td,cd->tc", x_low, qkv_heads, preferred_element_type=f32)
    positions = jnp.arange(seq, dtype=jnp.int32)
    cosine_table, sine_table = angles(positions, hd)
    turned = rotate(
        projected[:, : (heads + keys) * hd].reshape(seq, heads + keys, hd),
        cosine_table,
        sine_table,
    ).astype(bf16)
    query = turned[:, :heads].reshape(seq, keys, group, hd).transpose(1, 2, 0, 3)
    key = turned[:, heads:].transpose(1, 0, 2)
    value = (
        projected[:, (heads + keys) * hd :].astype(bf16).reshape(seq, keys, hd).transpose(1, 0, 2)
    )
    valid = (seg_all[:, None] == seg_all[None, :]) & (positions[None, :] <= positions[:, None])
    score = jnp.einsum("hgqd,hkd->hgqk", query, key, preferred_element_type=f32) * scale
    score = jnp.where(valid, score, negative_large)
    top = jnp.max(score, axis=-1, keepdims=True)
    weight = jnp.where(valid, jnp.exp(score - top), 0.0)
    prob = weight / jnp.sum(weight, axis=-1, keepdims=True)
    prob_low = prob.astype(bf16)
    attended = jnp.einsum("hgqk,hkd->hgqd", prob_low, value, preferred_element_type=f32)
    mixed_heads = attended.transpose(2, 0, 1, 3).reshape(seq, heads * hd).astype(bf16)
    mixed = lax.all_to_all(mixed_heads, "ep", split_axis=0, concat_axis=1, tiled=True)

    hidden_one = layer_in.astype(f32)
    for start, part in zip(spans, out_parts):
        piece = lax.dynamic_slice_in_dim(mixed, start, out_cols, 1)
        hidden_one = hidden_one + jnp.einsum("tc,dc->td", piece, part, preferred_element_type=f32)
    scale_two = lax.rsqrt(jnp.mean(hidden_one * hidden_one, axis=-1, keepdims=True) + eps)
    normed_two = hidden_one * scale_two
    x_two = (normed_two * gain_two).astype(bf16)
    x_two_all = lax.all_gather(x_two, "ep", axis=0, tiled=True)
    late_mixed, _ = lax.optimization_barrier((mixed, x_two))
    mixed_all = lax.all_gather(late_mixed, "ep", axis=0, tiled=True)

    logits = jnp.einsum("ed,td->et", full_router, x_two_all, preferred_element_type=f32)
    logits = jnp.where(chosen, logits, negative_large)
    raised = jnp.where(chosen, jnp.exp(logits - jnp.max(logits, axis=0, keepdims=True)), 0.0)
    gates = raised / jnp.sum(raised, axis=0, keepdims=True)
    own_gates = lax.dynamic_slice_in_dim(gates, me * mine, mine, 0)
    place_gate = jnp.sum(jnp.where(pick, own_gates[:, None, :], 0.0), axis=-1)[:, :, None]

    def gather(rows):
        picked = jnp.einsum("pt,td->pd", pick_low, rows, preferred_element_type=f32)
        return picked.astype(bf16).reshape(mine, capacity, width)

    def scatter(rows):
        back = jnp.einsum(
            "tp,pd->td", pick_back, rows.reshape(mine * capacity, width), preferred_element_type=f32
        )
        return back.astype(bf16)

    cols = width // copies

    def grad_rows(left, right, first):
        if not grp_direct(copies):
            part = jnp.einsum("jcf,jcd->jfd", left, right, preferred_element_type=f32)
            part = part.astype(bf16)
            return lax.psum_scatter(part, "grp", scatter_dimension=2, tiled=True).astype(f32)

        def block(step):
            return lax.dynamic_slice_in_dim(right, (at ^ step) * cols, cols, 2)

        if copies == 2:
            away, stay = block(1), block(0)
        else:
            second = 3 - first
            away = jnp.concatenate([block(first), block(3)], axis=2)
            stay = jnp.concatenate([block(0), block(second)], axis=2)
        away = jnp.einsum("jcf,jcd->jfd", left, away, preferred_element_type=f32).astype(bf16)
        got = grp_send(away, first, copies)
        kept = jnp.einsum("jcf,jcd->jfd", left, stay, preferred_element_type=f32)
        return kept, got

    def grad_finish(state, first):
        if not grp_direct(copies):
            return state
        kept, got = state
        total = kept + got.astype(f32)
        if copies == 2:
            return total
        passed = grp_send(total[:, :, cols:].astype(bf16), 3 - first, copies)
        return total[:, :, :cols] + passed.astype(f32)

    dense_g = gather(g_all)
    x_two_all, dense_g, pick_back = lax.optimization_barrier((x_two_all, dense_g, pick_back))
    dense_in = gather(x_two_all)
    pair_pre = jnp.einsum("jcd,jfd->jcf", dense_in, w_pair, preferred_element_type=f32)
    gate_pre, up_pre = pair_pre[:, :, :hidden], pair_pre[:, :, hidden:]
    logistic = jax.nn.sigmoid(gate_pre)
    inner = (gate_pre * logistic * up_pre).astype(bf16)
    expert_out = jnp.einsum("jcf,jfd->jcd", inner, w_down, preferred_element_type=f32)
    place_dgate = jnp.sum(expert_out * dense_g.astype(f32), axis=-1)
    dgate_own = jnp.sum(jnp.where(pick, place_dgate[:, :, None], 0.0), axis=1)
    dense_grad = (place_gate * dense_g.astype(f32)).astype(bf16)
    inner_grad = jnp.einsum("jcd,jfd->jcf", dense_grad, w_down, preferred_element_type=f32)
    gate_back = (inner_grad * up_pre * logistic * (1.0 + gate_pre * (1.0 - logistic))).astype(bf16)
    up_back = (inner_grad * gate_pre * logistic).astype(bf16)
    pair_back = jnp.concatenate([gate_back, up_back], axis=2)
    slot_grad = jnp.einsum("jcf,jfd->jcd", pair_back, w_pair, preferred_element_type=f32)
    back_part = scatter(slot_grad.astype(bf16))
    two_grad = lax.psum_scatter(back_part, "ep", scatter_dimension=0, tiled=True).astype(f32)
    dgate = lax.all_to_all(dgate_own, "ep", split_axis=1, concat_axis=0, tiled=True)
    half = hidden + hidden // 2
    down_state = grad_rows(inner, dense_grad, 1)
    pair_state = grad_rows(pair_back[:, :, :half], dense_in, 2)
    rest_state = grad_rows(pair_back[:, :, half:], dense_in, 1)
    out_part = scatter((place_gate * expert_out).astype(bf16))
    two_grad, out_part = lax.optimization_barrier((two_grad, out_part))
    returned = lax.psum_scatter(out_part, "ep", scatter_dimension=0, tiled=True)

    delta = out_cotangent.astype(f32)
    gates_here = lax.dynamic_slice_in_dim(gates, me * tokens, tokens, 1)
    chosen_grad = gates_here * (dgate - jnp.sum(gates_here * dgate, axis=0, keepdims=True))
    logit_grad = chosen_grad.astype(bf16)
    router_grad = jnp.einsum("et,td->ed", logit_grad, x_two, preferred_element_type=f32)
    two_grad = two_grad + jnp.einsum(
        "et,ed->td", logit_grad, full_router, preferred_element_type=f32
    )
    gain_two_grad = jnp.sum(two_grad * normed_two, axis=0, keepdims=True)
    hidden_grad = delta + norm_back(two_grad, normed_two, scale_two, gain_two)
    hidden_low = hidden_grad.astype(bf16)
    mixing = jnp.stack(
        [
            jnp.einsum("td,dc->tc", hidden_low, part, preferred_element_type=f32).astype(bf16)
            for part in out_parts
        ]
    )
    mixing = mixing[ordered].transpose(1, 0, 2).reshape(tokens, -1)
    mixing_heads = lax.all_to_all(mixing, "ep", split_axis=1, concat_axis=0, tiled=True)
    hidden_cols = lax.all_to_all(hidden_low, "ep", split_axis=1, concat_axis=0, tiled=True)

    change = mixing_heads.reshape(seq, keys, group, hd).transpose(1, 2, 0, 3)
    prob_grad = jnp.einsum("hgqd,hkd->hgqk", change, value, preferred_element_type=f32)
    row = jnp.sum(prob * prob_grad, axis=-1, keepdims=True)
    score_grad = (prob * (prob_grad - row)).astype(bf16)
    value_grad = jnp.einsum("hgqk,hgqd->hkd", prob_low, change, preferred_element_type=f32)
    query_grad = jnp.einsum("hgqk,hkd->hgqd", score_grad, key, preferred_element_type=f32) * scale
    key_grad = jnp.einsum("hgqk,hgqd->hkd", score_grad, query, preferred_element_type=f32) * scale
    turned_grad = jnp.concatenate(
        [
            query_grad.transpose(2, 0, 1, 3).reshape(seq, heads, hd),
            key_grad.transpose(1, 0, 2),
        ],
        axis=1,
    )
    turned_grad = rotate(turned_grad, cosine_table, -sine_table).reshape(seq, (heads + keys) * hd)
    proj_grad = jnp.concatenate(
        [turned_grad, value_grad.transpose(1, 0, 2).reshape(seq, keys * hd)], axis=1
    ).astype(bf16)
    one_part = jnp.einsum("tc,cd->td", proj_grad, qkv_heads, preferred_element_type=f32)
    gain_one_grad = jnp.sum(one_part * normed_all, axis=0, keepdims=True)
    one_grad = lax.psum_scatter(
        one_part.astype(bf16), "ep", scatter_dimension=0, tiled=True
    ).astype(f32)
    proj_rows = move_blocks(
        proj_grad.T.reshape(slots, block_rows, seq), pick_head, to_rows, order_row
    ).reshape(slots * block_rows, seq)
    qkv_grad = jnp.einsum("ct,td->cd", proj_rows, x_low, preferred_element_type=f32)
    out_grad = jnp.einsum("td,tc->dc", hidden_cols, mixed_all, preferred_element_type=f32)

    gain_pack = jnp.concatenate([gain_one_grad, gain_two_grad], axis=0)
    gain_pack = gain_pack.reshape(2, devices, gain_width).transpose(1, 0, 2)
    gain_pack = gain_pack.reshape(devices, 1, 2 * gain_width)
    gain_pack = jnp.pad(gain_pack, ((0, 0), (0, 0), (0, width - 2 * gain_width)))
    small_pack = jnp.concatenate([router_grad.reshape(devices, mine, width), gain_pack], axis=1)
    small_pack = lax.all_to_all(small_pack, "ep", split_axis=0, concat_axis=0, tiled=True)
    small_part = jnp.sum(small_pack, axis=0)
    if copies == mine + 1 and grp_direct(copies):
        per_copy = [
            qkv_grad.astype(bf16).reshape(copies, -1, width),
            out_grad.astype(bf16).reshape(copies, -1, width),
            jnp.pad(small_part.astype(bf16)[:, None], ((0, 0), (0, 7), (0, 0))),
        ]
        sizes = [part.shape[1] for part in per_copy]
        sums = grp_all_sum(
            jnp.concatenate(per_copy, axis=1).reshape(-1, width), copies, at
        ).reshape(copies, -1, width)
        qkv_sum = sums[:, : sizes[0]].reshape(-1, width)
        out_sum = sums[:, sizes[0] : sizes[0] + sizes[1]].reshape(-1, width)
        small_sum = sums[:, sizes[0] + sizes[1]]
    else:
        qkv_sum = grp_all_sum(qkv_grad.astype(bf16), copies, at)
        out_sum = grp_all_sum(out_grad.astype(bf16), copies, at)
        small_sum = grp_total(small_part, copies)
    down_sum = grad_finish(down_state, 1)
    pair_sum = grad_finish(pair_state, 2)
    rest_sum = grad_finish(rest_state, 1)

    layer_out = (hidden_one + returned.astype(f32)).astype(bf16)
    residual = layer_in.astype(f32)
    scale_one = lax.rsqrt(jnp.mean(residual * residual, axis=-1, keepdims=True) + eps)
    grad_in = (hidden_grad + norm_back(one_grad, residual * scale_one, scale_one, gain_one)).astype(
        bf16
    )
    return (
        layer_out,
        grad_in,
        qkv_sum,
        out_sum,
        small_sum[:mine],
        small_sum[mine, :gain_width],
        small_sum[mine, gain_width : 2 * gain_width],
        pair_sum[:, :hidden],
        jnp.concatenate([pair_sum[:, hidden:], rest_sum], axis=1),
        down_sum,
    )


def solution(mesh):
    in_specs = (
        P(("grp", "ep"), None),
        P(("grp", "ep")),
        P(("grp", "ep"), None),
        P("ep", None),
        P("ep", None),
        P("ep", None),
        P("ep"),
        P("ep"),
        P("ep", None, None),
        P("ep", None, None),
        P("ep", None, None),
        P(("grp", "ep"), None),
    )
    out_specs = (
        P(("grp", "ep"), None),
        P(("grp", "ep"), None),
        P("ep", None),
        P("ep", None),
        P("ep", None),
        P("ep"),
        P("ep"),
        P("ep", None, "grp"),
        P("ep", None, "grp"),
        P("ep", None, "grp"),
    )

    return jax.shard_map(local, mesh=mesh, in_specs=in_specs, out_specs=out_specs, check_vma=False)
```

```python
import jax
import jax.numpy as jnp
from jax import lax
from jax.sharding import PartitionSpec as P


QUERY_HEADS = 24
KEY_VALUE_HEADS = 8
HEAD_DIMENSION = 64
TOPK = 8


eps = 1e-06
theta = 10000.0
negative_large = -1e30
f32 = jnp.float32
bf16 = jnp.bfloat16


def angles(token_positions, head_size):
    half = head_size // 2
    freq = theta ** (-jnp.arange(half, dtype=f32) * 2.0 / head_size)
    angle = token_positions.astype(f32)[:, None] * freq[None, :]
    return (jnp.cos(angle)[:, None, :], jnp.sin(angle)[:, None, :])


def rotate(value_matrix, cosine_table, sine_table):
    half = value_matrix.shape[-1] // 2
    first = value_matrix[..., :half]
    second = value_matrix[..., half:]
    return jnp.concatenate(
        [
            first * cosine_table - second * sine_table,
            second * cosine_table + first * sine_table,
        ],
        axis=-1,
    )


def norm_back(delta, normed, scale, gain):
    scaled = delta * gain
    return scale * (scaled - normed * jnp.mean(scaled * normed, axis=-1, keepdims=True))


def head_plan(devices):
    per_query = QUERY_HEADS // devices
    per_key = KEY_VALUE_HEADS // devices
    blocks = QUERY_HEADS + 2 * KEY_VALUE_HEADS
    own = blocks // devices

    def place(block):
        if block < QUERY_HEADS:
            return block // per_query, block % per_query
        block -= QUERY_HEADS
        if block < KEY_VALUE_HEADS:
            return block // per_key, per_query + block % per_key
        block -= KEY_VALUE_HEADS
        return block // per_key, per_query + per_key + block % per_key

    left = [[(s, *place(i * own + s)) for s in range(own)] for i in range(devices)]
    rounds = []
    for _ in range(own):
        taken = {}

        def assign(i, seen):
            for edge in left[i]:
                j = edge[1]
                if j in seen:
                    continue
                seen.add(j)
                if j not in taken or assign(taken[j][0], seen):
                    taken[j] = (i, edge)
                    return True
            return False

        for i in range(devices):
            assign(i, set())
        source_slot, target, target_slot = [0] * devices, [0] * devices, [0] * devices
        for j, (i, edge) in taken.items():
            source_slot[i], target[i], target_slot[j] = edge[0], j, edge[2]
            left[i].remove(edge)
        rounds.append((source_slot, target, target_slot))
    return rounds


def move_blocks(blocks, pick, pairs, order):
    chosen = blocks[pick]
    return jnp.stack([lax.ppermute(chosen[p], "ep", pair) for p, pair in enumerate(pairs)])[order]


def grp_direct(copies):
    return copies in (2, 4)


def grp_send(value, step, copies):
    return lax.ppermute(value, "grp", [(a, a ^ step) for a in range(copies)])


def grp_gather(block, copies, at):
    if not grp_direct(copies):
        return lax.all_gather(block, "grp", axis=0, tiled=False)
    got = jnp.stack([block] + [grp_send(block, d, copies) for d in range(1, copies)])
    return got[jnp.arange(copies, dtype=jnp.int32) ^ at]


def grp_total(value, copies):
    if not grp_direct(copies):
        return lax.psum(value, "grp")
    return value + sum(grp_send(value, d, copies) for d in range(1, copies))


def grp_all_sum(rows, copies, at):
    if not grp_direct(copies):
        return lax.psum(rows, "grp").astype(f32)
    blocks = rows.reshape(copies, rows.shape[0] // copies, rows.shape[1])
    total = lax.dynamic_index_in_dim(blocks, at, 0, keepdims=False).astype(f32)
    for d in range(1, copies):
        part = lax.dynamic_index_in_dim(blocks, at ^ d, 0, keepdims=False)
        total = total + grp_send(part, d, copies).astype(f32)
    return grp_gather(total.astype(bf16), copies, at).reshape(rows.shape).astype(f32)


def local(
    layer_in,
    segments,
    routes,
    qkv_weight,
    out_weight,
    router_weight,
    norm1_gain,
    norm2_gain,
    w_gate,
    w_up,
    w_down,
    out_cotangent,
):
    tokens, width = layer_in.shape
    devices = lax.axis_size("ep")
    me = lax.axis_index("ep")
    copies = lax.axis_size("grp")
    at = lax.axis_index("grp")
    mine = w_gate.shape[0]
    hidden = w_gate.shape[1]
    experts = mine * devices
    seq = tokens * devices
    capacity = 9 * tokens * TOPK // (8 * mine)
    heads = QUERY_HEADS // devices
    keys = KEY_VALUE_HEADS // devices
    group = heads // keys
    hd = HEAD_DIMENSION
    scale = hd ** (-0.5)

    x_all = lax.all_gather(layer_in, "ep", axis=0, tiled=True)
    gain_width = norm1_gain.shape[0]
    small = jnp.concatenate(
        [
            router_weight.reshape(-1),
            norm1_gain,
            norm2_gain,
            routes.T.astype(bf16).reshape(-1),
            segments.astype(bf16),
        ]
    )
    small_all = lax.all_gather(small, "ep", axis=0, tiled=False)
    cut = mine * width
    full_router = small_all[:, :cut].reshape(experts, width)
    gain_one = small_all[:, cut : cut + gain_width].reshape(1, width).astype(f32)
    gain_two = small_all[:, cut + gain_width : cut + 2 * gain_width].reshape(1, width).astype(f32)
    cut += 2 * gain_width
    routes_all = small_all[:, cut : cut + tokens * TOPK].reshape(devices, TOPK, tokens)
    routes_all = routes_all.transpose(1, 0, 2).reshape(TOPK, seq).astype(jnp.int32)
    seg_all = small_all[:, cut + tokens * TOPK :].reshape(seq)

    rounds = head_plan(devices)
    slots = len(rounds)
    to_heads = [[(i, t[i]) for i in range(devices)] for _, t, _ in rounds]
    to_rows = [[(b, a) for a, b in pair] for pair in to_heads]
    table = []
    for d in range(devices):
        put = [[r[2][d] for r in rounds].index(s) for s in range(slots)]
        back = [[r[0][d] for r in rounds].index(s) for s in range(slots)]
        table.append([r[0][d] for r in rounds] + [r[2][d] for r in rounds] + put + back)
    row = jnp.array(table, jnp.int32)[me]
    pick_row, pick_head, order_head, order_row = (
        row[n * slots : (n + 1) * slots] for n in range(4)
    )
    block_rows = qkv_weight.shape[0] // slots
    late_qkv, _ = lax.optimization_barrier((qkv_weight, small_all))
    qkv_heads = move_blocks(
        late_qkv.reshape(slots, block_rows, width), pick_row, to_heads, order_head
    ).reshape(slots * block_rows, width)
    if grp_direct(copies):
        out_cols = out_weight.shape[1] // copies
        out_quarter = lax.dynamic_slice_in_dim(out_weight, at * out_cols, out_cols, 1)
        out_quarter = lax.all_gather(out_quarter, "ep", axis=0, tiled=True)
        out_parts = None
        spans = [(at ^ d) * out_cols for d in range(copies)]
        ordered = jnp.arange(copies, dtype=jnp.int32) ^ at
    else:
        out_cols = out_weight.shape[1]
        out_quarter = lax.all_gather(out_weight, "ep", axis=0, tiled=True)
        spans = [0]
        ordered = jnp.zeros((1,), jnp.int32)

    late_cotangent, _ = lax.optimization_barrier((out_cotangent, x_all))
    g_all = lax.all_gather(late_cotangent, "ep", axis=0, tiled=True)

    expert_row = jnp.arange(experts, dtype=jnp.int32)[:, None, None]
    chosen = jnp.any(routes_all[None] == expert_row, axis=1)
    own_chosen = lax.dynamic_slice_in_dim(chosen, me * mine, mine, 0)
    before = (
        jnp.arange(seq, dtype=jnp.int32)[:, None] < jnp.arange(seq, dtype=jnp.int32)[None, :]
    ).astype(bf16)
    rank = jnp.einsum(
        "es,st->et", own_chosen.astype(bf16), before, preferred_element_type=f32
    ).astype(jnp.int32)
    rank = jnp.where(own_chosen, rank, -1)
    places = jnp.arange(capacity, dtype=jnp.int32)[None, :, None]
    pick = rank[:, None, :] == places
    pick_low = pick.astype(bf16).reshape(mine * capacity, seq)
    pick_back = (rank.T[:, :, None] == jnp.arange(capacity, dtype=jnp.int32)[None, None, :]).astype(
        bf16
    )
    pick_back = pick_back.reshape(seq, mine * capacity)

    residual_all = x_all.astype(f32)
    scale_one_all = lax.rsqrt(jnp.mean(residual_all * residual_all, axis=-1, keepdims=True) + eps)
    normed_all = residual_all * scale_one_all
    x_low = (normed_all * gain_one).astype(bf16)
    projected = jnp.einsum("td,cd->tc", x_low, qkv_heads, preferred_element_type=f32)
    positions = jnp.arange(seq, dtype=jnp.int32)
    cosine_table, sine_table = angles(positions, hd)
    turned = rotate(
        projected[:, : (heads + keys) * hd].reshape(seq, heads + keys, hd),
        cosine_table,
        sine_table,
    ).astype(bf16)
    query = turned[:, :heads].reshape(seq, keys, group, hd).transpose(1, 2, 0, 3)
    key = turned[:, heads:].transpose(1, 0, 2)
    value = (
        projected[:, (heads + keys) * hd :].astype(bf16).reshape(seq, keys, hd).transpose(1, 0, 2)
    )
    valid = (seg_all[:, None] == seg_all[None, :]) & (positions[None, :] <= positions[:, None])
    score = jnp.einsum("hgqd,hkd->hgqk", query, key, preferred_element_type=f32) * scale
    score = jnp.where(valid, score, negative_large)
    top = jnp.max(score, axis=-1, keepdims=True)
    weight = jnp.where(valid, jnp.exp(score - top), 0.0)
    prob = weight / jnp.sum(weight, axis=-1, keepdims=True)
    prob_low = prob.astype(bf16)
    attended = jnp.einsum("hgqk,hkd->hgqd", prob_low, value, preferred_element_type=f32)
    mixed_heads = attended.transpose(2, 0, 1, 3).reshape(seq, heads * hd).astype(bf16)
    mixed = lax.all_to_all(mixed_heads, "ep", split_axis=0, concat_axis=1, tiled=True)
    if grp_direct(copies):
        out_quarter, _ = lax.optimization_barrier((out_quarter, mixed_heads))
        out_parts = [out_quarter] + [
            grp_send(out_quarter, d, copies) for d in range(1, min(copies, 3))
        ]
        if copies == 4:
            mid = out_quarter.shape[0] // 2
            upper = grp_send(out_parts[1][:mid], 2, copies)
            lower = grp_send(out_parts[2][mid:], 1, copies)
            out_parts.append(jnp.concatenate([upper, lower], axis=0))
    else:
        out_parts = [out_quarter]

    hidden_one = layer_in.astype(f32)
    for start, part in zip(spans, out_parts):
        piece = lax.dynamic_slice_in_dim(mixed, start, out_cols, 1)
        hidden_one = hidden_one + jnp.einsum("tc,dc->td", piece, part, preferred_element_type=f32)
    scale_two = lax.rsqrt(jnp.mean(hidden_one * hidden_one, axis=-1, keepdims=True) + eps)
    normed_two = hidden_one * scale_two
    x_two = (normed_two * gain_two).astype(bf16)
    x_two_all = lax.all_gather(x_two, "ep", axis=0, tiled=True)
    late_mixed, _ = lax.optimization_barrier((mixed, x_two))
    mixed_all = lax.all_gather(late_mixed, "ep", axis=0, tiled=True)

    logits = jnp.einsum("ed,td->et", full_router, x_two_all, preferred_element_type=f32)
    logits = jnp.where(chosen, logits, negative_large)
    raised = jnp.where(chosen, jnp.exp(logits - jnp.max(logits, axis=0, keepdims=True)), 0.0)
    gates = raised / jnp.sum(raised, axis=0, keepdims=True)
    own_gates = lax.dynamic_slice_in_dim(gates, me * mine, mine, 0)
    place_gate = jnp.sum(jnp.where(pick, own_gates[:, None, :], 0.0), axis=-1)[:, :, None]

    def gather(rows):
        picked = jnp.einsum("pt,td->pd", pick_low, rows, preferred_element_type=f32)
        return picked.astype(bf16).reshape(mine, capacity, width)

    def scatter(rows):
        back = jnp.einsum(
            "tp,pd->td", pick_back, rows.reshape(mine * capacity, width), preferred_element_type=f32
        )
        return back.astype(bf16)

    cols = width // copies

    def grad_rows(left, right, first):
        if not grp_direct(copies):
            part = jnp.einsum("jcf,jcd->jfd", left, right, preferred_element_type=f32)
            part = part.astype(bf16)
            return lax.psum_scatter(part, "grp", scatter_dimension=2, tiled=True).astype(f32)

        def block(step):
            return lax.dynamic_slice_in_dim(right, (at ^ step) * cols, cols, 2)

        if copies == 2:
            away, stay = block(1), block(0)
        else:
            second = 3 - first
            away = jnp.concatenate([block(first), block(3)], axis=2)
            stay = jnp.concatenate([block(0), block(second)], axis=2)
        away = jnp.einsum("jcf,jcd->jfd", left, away, preferred_element_type=f32).astype(bf16)
        got = grp_send(away, first, copies)
        kept = jnp.einsum("jcf,jcd->jfd", left, stay, preferred_element_type=f32)
        return kept, got

    def grad_finish(state, first):
        if not grp_direct(copies):
            return state
        kept, got = state
        total = kept + got.astype(f32)
        if copies == 2:
            return total
        passed = grp_send(total[:, :, cols:].astype(bf16), 3 - first, copies)
        return total[:, :, :cols] + passed.astype(f32)

    dense_g = gather(g_all)
    x_two_all, dense_g, pick_back = lax.optimization_barrier((x_two_all, dense_g, pick_back))
    dense_in = gather(x_two_all)
    gate_pre = jnp.einsum("jcd,jfd->jcf", dense_in, w_gate, preferred_element_type=f32)
    up_pre = jnp.einsum("jcd,jfd->jcf", dense_in, w_up, preferred_element_type=f32)
    logistic = jax.nn.sigmoid(gate_pre)
    inner = (gate_pre * logistic * up_pre).astype(bf16)
    expert_out = jnp.einsum("jcf,jfd->jcd", inner, w_down, preferred_element_type=f32)
    place_dgate = jnp.sum(expert_out * dense_g.astype(f32), axis=-1)
    dgate_own = jnp.sum(jnp.where(pick, place_dgate[:, :, None], 0.0), axis=1)
    dense_grad = (place_gate * dense_g.astype(f32)).astype(bf16)
    inner_grad = jnp.einsum("jcd,jfd->jcf", dense_grad, w_down, preferred_element_type=f32)
    gate_back = (inner_grad * up_pre * logistic * (1.0 + gate_pre * (1.0 - logistic))).astype(bf16)
    up_back = (inner_grad * gate_pre * logistic).astype(bf16)
    slot_grad = jnp.einsum(
        "jcf,jfd->jcd", gate_back, w_gate, preferred_element_type=f32
    ) + jnp.einsum("jcf,jfd->jcd", up_back, w_up, preferred_element_type=f32)
    back_part = scatter(slot_grad.astype(bf16))
    two_grad = lax.psum_scatter(back_part, "ep", scatter_dimension=0, tiled=True).astype(f32)
    dgate = lax.all_to_all(dgate_own, "ep", split_axis=1, concat_axis=0, tiled=True)
    half = hidden // 2
    pair_back = jnp.concatenate([gate_back, up_back[:, :, :half]], axis=2)
    down_state = grad_rows(inner, dense_grad, 1)
    pair_state = grad_rows(pair_back, dense_in, 2)
    rest_state = grad_rows(up_back[:, :, half:], dense_in, 1)
    out_part = scatter((place_gate * expert_out).astype(bf16))
    states = (down_state, pair_state, rest_state)
    if grp_direct(copies):
        kepts = tuple(state[0] for state in states)
        two_grad, out_part, kepts = lax.optimization_barrier((two_grad, out_part, kepts))
        gots = tuple(state[1] for state in states)
    else:
        two_grad, out_part = lax.optimization_barrier((two_grad, out_part))
    delta = out_cotangent.astype(f32)
    gates_here = lax.dynamic_slice_in_dim(gates, me * tokens, tokens, 1)
    chosen_grad = gates_here * (dgate - jnp.sum(gates_here * dgate, axis=0, keepdims=True))
    logit_grad = chosen_grad.astype(bf16)
    router_grad = jnp.einsum("et,td->ed", logit_grad, x_two, preferred_element_type=f32)
    two_grad = two_grad + jnp.einsum(
        "et,ed->td", logit_grad, full_router, preferred_element_type=f32
    )
    gain_two_grad = jnp.sum(two_grad * normed_two, axis=0, keepdims=True)
    hidden_grad = delta + norm_back(two_grad, normed_two, scale_two, gain_two)
    hidden_low = hidden_grad.astype(bf16)
    mixing = jnp.stack(
        [
            jnp.einsum("td,dc->tc", hidden_low, part, preferred_element_type=f32).astype(bf16)
            for part in out_parts
        ]
    )
    mixing = mixing[ordered].transpose(1, 0, 2).reshape(tokens, -1)
    both = jnp.concatenate(
        [mixing.reshape(tokens, devices, -1), hidden_low.reshape(tokens, devices, -1)], axis=2
    )
    both = lax.all_to_all(both.transpose(1, 0, 2), "ep", split_axis=0, concat_axis=0, tiled=True)
    both, out_part = lax.optimization_barrier((both, out_part))
    returned = lax.psum_scatter(out_part, "ep", scatter_dimension=0, tiled=True)
    both = both.reshape(seq, -1)
    mixing_heads, hidden_cols = both[:, : heads * hd], both[:, heads * hd :]

    change = mixing_heads.reshape(seq, keys, group, hd).transpose(1, 2, 0, 3)
    prob_grad = jnp.einsum("hgqd,hkd->hgqk", change, value, preferred_element_type=f32)
    row = jnp.sum(prob * prob_grad, axis=-1, keepdims=True)
    score_grad = (prob * (prob_grad - row)).astype(bf16)
    value_grad = jnp.einsum("hgqk,hgqd->hkd", prob_low, change, preferred_element_type=f32)
    query_grad = jnp.einsum("hgqk,hkd->hgqd", score_grad, key, preferred_element_type=f32) * scale
    key_grad = jnp.einsum("hgqk,hgqd->hkd", score_grad, query, preferred_element_type=f32) * scale
    turned_grad = jnp.concatenate(
        [
            query_grad.transpose(2, 0, 1, 3).reshape(seq, heads, hd),
            key_grad.transpose(1, 0, 2),
        ],
        axis=1,
    )
    turned_grad = rotate(turned_grad, cosine_table, -sine_table).reshape(seq, (heads + keys) * hd)
    proj_grad = jnp.concatenate(
        [turned_grad, value_grad.transpose(1, 0, 2).reshape(seq, keys * hd)], axis=1
    ).astype(bf16)
    one_part = jnp.einsum("tc,cd->td", proj_grad, qkv_heads, preferred_element_type=f32)
    gain_one_grad = jnp.sum(one_part * normed_all, axis=0, keepdims=True)
    one_grad = lax.psum_scatter(
        one_part.astype(bf16), "ep", scatter_dimension=0, tiled=True
    ).astype(f32)
    proj_rows = move_blocks(
        proj_grad.T.reshape(slots, block_rows, seq), pick_head, to_rows, order_row
    ).reshape(slots * block_rows, seq)
    qkv_grad = jnp.einsum("ct,td->cd", proj_rows, x_low, preferred_element_type=f32)
    out_grad = jnp.einsum("td,tc->dc", hidden_cols, mixed_all, preferred_element_type=f32)

    gain_pack = jnp.concatenate([gain_one_grad, gain_two_grad], axis=0)
    gain_pack = gain_pack.reshape(2, devices, gain_width).transpose(1, 0, 2)
    gain_pack = gain_pack.reshape(devices, 1, 2 * gain_width)
    gain_pack = jnp.pad(gain_pack, ((0, 0), (0, 0), (0, width - 2 * gain_width)))
    small_pack = jnp.concatenate([router_grad.reshape(devices, mine, width), gain_pack], axis=1)
    small_pack = lax.all_to_all(small_pack, "ep", split_axis=0, concat_axis=0, tiled=True)
    small_part = jnp.sum(small_pack, axis=0)
    out_sum = grp_all_sum(out_grad.astype(bf16), copies, at)
    small_sum = grp_total(small_part, copies)
    qkv_sum = grp_all_sum(qkv_grad.astype(bf16), copies, at)
    if grp_direct(copies):
        gots, _ = lax.optimization_barrier((gots, proj_grad))
        states = tuple(zip(kepts, gots))
    down_sum = grad_finish(states[0], 1)
    pair_sum = grad_finish(states[1], 2)
    rest_sum = grad_finish(states[2], 1)

    layer_out = (hidden_one + returned.astype(f32)).astype(bf16)
    residual = layer_in.astype(f32)
    scale_one = lax.rsqrt(jnp.mean(residual * residual, axis=-1, keepdims=True) + eps)
    grad_in = (hidden_grad + norm_back(one_grad, residual * scale_one, scale_one, gain_one)).astype(
        bf16
    )
    return (
        layer_out,
        grad_in,
        qkv_sum,
        out_sum,
        small_sum[:mine],
        small_sum[mine, :gain_width],
        small_sum[mine, gain_width : 2 * gain_width],
        pair_sum[:, :hidden],
        jnp.concatenate([pair_sum[:, hidden:], rest_sum], axis=1),
        down_sum,
    )


def solution(mesh):
    in_specs = (
        P(("grp", "ep"), None),
        P(("grp", "ep")),
        P(("grp", "ep"), None),
        P("ep", None),
        P("ep", None),
        P("ep", None),
        P("ep"),
        P("ep"),
        P("ep", None, None),
        P("ep", None, None),
        P("ep", None, None),
        P(("grp", "ep"), None),
    )
    out_specs = (
        P(("grp", "ep"), None),
        P(("grp", "ep"), None),
        P("ep", None),
        P("ep", None),
        P("ep", None),
        P("ep"),
        P("ep"),
        P("ep", None, "grp"),
        P("ep", None, "grp"),
        P("ep", None, "grp"),
    )

    return jax.shard_map(local, mesh=mesh, in_specs=in_specs, out_specs=out_specs, check_vma=False)
```
